256 devices in a mesh: ctx: 4 (over x), head: 16 (over y, z_hi), seq: 4 (over z_lo, core).
Axes of the slice: x: 4, y: 4, z: 8 (z_hi: 4, z_lo: 2; z = z_hi * 2 + z_lo), core: 2. Of those that a mesh axis runs over, the one named last changes fastest.
Arguments:
- stretch_slot: int32 [32], P('seq'), parts along dimension 0, may hold values from 0 to 7, as said below
- gate_in: bfloat16 [2048, 8192], P(('seq', 'ctx'), 'head'), parts along dimension 0, may hold values from -6 to 6
- conv_in: bfloat16 [2048, 8192], P(('seq', 'ctx'), 'head'), parts along dimension 0, may hold values from -6 to 6
- value_in: bfloat16 [2048, 8192], P(('seq', 'ctx'), 'head'), parts along dimension 0, may hold values from -6 to 6
- modal_rate: float32 [64, 8192], P('seq', 'head'), parts along dimension 0, may hold values from 0.00048828125 to 0.05
- modal_residue: float32 [64, 8192], P('seq', 'head'), parts along dimension 0, may hold values from -0.078125 to 0.078125
- skip_gain: float32 [32768], P(('seq', 'head')), parts along dimension 0, may hold values from -4 to 4
- query_proj: bfloat16 [2048, 8192], P(('seq', 'ctx'), 'head'), parts along dimension 0, may hold values from -1024 to 1024
- key_proj: bfloat16 [2048, 8192], P(('seq', 'ctx'), 'head'), parts along dimension 0, may hold values from -256 to 256
- value_proj: bfloat16 [2048, 8192], P(('seq', 'ctx'), 'head'), parts along dimension 0, may hold values from -6 to 6
- out_weight: bfloat16 [32768, 8192], P(('seq', 'head')), parts along dimension 0, may hold values from -0.09375 to 0.09375
Outputs:
- mixed: bfloat16 [2048, 8192], P(('seq', 'ctx'), 'head'), parts along dimension 0
The draws below stay inside these ranges and needn't reach their ends.
There are 4 independent parts, one for each index of `seq`. The reference program is written for one: setup_inputs(seed, part) draws one part's arguments, and reference() takes and returns one part's arrays. A program takes and returns all parts, laid end to end along the dimension named above; each array names one. Nothing has to cross between parts.
Inputs may be any that keep to these rules, and one draw needn't show every extreme that they name: Slot s holds stretch stretch_slot[s]; every stretch number appears exactly once.
All inputs are finite; a program needn't handle non-finite values.
Results may differ from the reference program's by a relative error of at most 0.015.
Values may be sent and summed in bfloat16 or wider, within the bound.
No kernel may reach another device: no remote copies, remote signals or barrier semaphores. Data moves between devices by JAX's collectives and lax.ppermute only.
A program may use at most 128 MiB of HBM per device.

```python
import math
import jax
import jax.numpy as jnp
from jax import lax

D = 8192
HEADS = 64
N_MODE = 16
CH = 64
SEQ_LEN = 512
N_CTX = 4


def order_stretches(key):
    return jax.random.permutation(jax.random.fold_in(key, 11), 2 * N_CTX).astype(jnp.int32)


def draw_stretch_slot(key, part):
    return order_stretches(key)


def attention_inputs(key):
    query_key = jax.random.fold_in(key, 21)
    keys_key = jax.random.fold_in(key, 22)
    queries = 2.0 * jax.random.normal(query_key, (SEQ_LEN, D), jnp.float32)
    key_rows = jax.random.normal(keys_key, (SEQ_LEN, D), jnp.float32)
    return (queries, key_rows)


def draw_query_proj(key, part):
    queries, key_rows = attention_inputs(key)
    return queries.astype(jnp.bfloat16)


def draw_key_proj(key, part):
    queries, key_rows = attention_inputs(key)
    return key_rows.astype(jnp.bfloat16)


def with_spikes(result, key, source, target, blocks, factor):
    owner, partner = [(jnp.arange(result.shape[axis_at]) // (result.shape[axis_at] // blocks)).reshape([-1 if axis == axis_at else 1 for axis in range(result.ndim)]) for axis_at in (source, target)]
    chosen = jax.random.permutation(key, blocks)[partner]
    strong = (owner == chosen) | (owner == (partner + blocks // 2) % blocks)
    return jnp.where(strong, factor * result, result)


def block_levels(own_key, extent, split, low, high):
    factor_of, own = 1.0, jax.random.fold_in(own_key, 6)
    for axis_at, shards_of in split:
        heights = jnp.exp(jax.random.uniform(jax.random.fold_in(own, axis_at), (shards_of,), jnp.float32, low / len(split), high / len(split)))
        factor_of = factor_of * jnp.repeat(heights, extent[axis_at] // shards_of).reshape([-1 if axis == axis_at else 1 for axis in range(len(extent))])
    return factor_of


def noise(own_key, extent, spread, reach, cuts=(), kind=jnp.bfloat16):
    drawn = jax.random.normal(own_key, extent, jnp.float32) * spread
    if len(cuts) > 0:
        drawn = block_levels(own_key, extent, cuts, -0.22, 0.18) * drawn
    return jnp.clip(drawn, min=-reach, max=reach).astype(kind)


def heavy_noise(own_key, dims, spread, reach, shards, heavy, kind=jnp.bfloat16):
    entries = spread * jax.random.normal(own_key, dims, jnp.float32)
    if shards:
        entries = entries * block_levels(own_key, dims, shards, -0.22, 0.18)
    return jnp.clip(with_spikes(entries, jax.random.fold_in(own_key, 3), *heavy), -reach, reach).astype(kind)


def setup_inputs(seed: int = 0, part: int = 0) -> dict:
    splits = jax.random.split(jax.random.key(seed), 12)
    own_keys = jax.random.split(jax.random.fold_in(splits[11], part), 12)
    return {
        "stretch_slot": draw_stretch_slot(jax.random.fold_in(jax.random.fold_in(splits[11], part), 71), part),
        "gate_in": noise(own_keys[1], (SEQ_LEN, D), 1.0, 6.0, ((0, 4), (1, 16))),
        "conv_in": noise(own_keys[2], (SEQ_LEN, D), 1.0, 6.0, ((0, 4), (1, 16))),
        "value_in": noise(own_keys[3], (SEQ_LEN, D), 1.0, 6.0, ((0, 4), (1, 16))),
        "modal_rate": jnp.clip(jnp.exp(math.log(0.05) - 4.6288867 * jax.random.uniform(own_keys[4], (N_MODE, D), jnp.float32) ** block_levels(own_keys[4], (N_MODE, D), ((1, 16),), -0.2, 0.2)), 0.00048828125, 0.05),
        "modal_residue": noise(own_keys[5], (N_MODE, D), 0.005, 0.078125, ((1, 16),), jnp.float32),
        "skip_gain": noise(own_keys[6], (D,), 0.3, 4.0, ((0, 16),), jnp.float32),
        "query_proj": draw_query_proj(jax.random.fold_in(jax.random.fold_in(splits[11], part), 71), part),
        "key_proj": draw_key_proj(jax.random.fold_in(jax.random.fold_in(splits[11], part), 71), part),
        "value_proj": noise(own_keys[9], (SEQ_LEN, D), 1.0, 6.0, ((0, 4), (1, 16))),
        "out_weight": heavy_noise(own_keys[10], (D, D), D ** -0.5, 0.09375, ((0, 16),), (0, 1, 16, 2.0)),
    }


def to_natural(array, inverse):
    blocks = array.reshape(2 * N_CTX, CH, array.shape[1])
    return blocks[inverse].reshape(SEQ_LEN, array.shape[1])

def reference(stretch_slot, gate_in, conv_in, value_in, modal_rate, modal_residue, skip_gain, query_proj, key_proj, value_proj, out_weight):
    slot_ids = jnp.arange(2 * N_CTX, dtype=jnp.int32)
    inverse = jnp.zeros((2 * N_CTX,), jnp.int32).at[stretch_slot].set(slot_ids)
    gate_float = to_natural(gate_in, inverse).astype(jnp.float32)
    product_in = to_natural(conv_in, inverse).astype(jnp.float32) * to_natural(value_in, inverse).astype(jnp.float32)
    offsets = jnp.arange(SEQ_LEN).astype(jnp.float32)

    def add_mode(filter_taps, mode_rows):
        rate_row, residue_row = mode_rows
        return (filter_taps + residue_row[None, :] * jnp.exp(-rate_row[None, :] * offsets[:, None]), None)
    filter_taps, unused_out = lax.scan(add_mode, jnp.zeros((SEQ_LEN, D), jnp.float32), (modal_rate, modal_residue))
    spectrum = jnp.fft.rfft(product_in, n=2 * SEQ_LEN, axis=0) * jnp.fft.rfft(filter_taps, n=2 * SEQ_LEN, axis=0)
    convolved = jnp.fft.irfft(spectrum, n=2 * SEQ_LEN, axis=0)[:SEQ_LEN].astype(jnp.float32)
    hyena_out = gate_float * (convolved + skip_gain[None, :] * product_in)
    head_size = D // HEADS
    score_scale = 1.0 / math.sqrt(head_size)
    query_heads = to_natural(query_proj, inverse).reshape(SEQ_LEN, HEADS, head_size).transpose(1, 0, 2)
    key_heads = to_natural(key_proj, inverse).reshape(SEQ_LEN, HEADS, head_size).transpose(1, 0, 2)
    value_heads = to_natural(value_proj, inverse).reshape(SEQ_LEN, HEADS, head_size).transpose(1, 0, 2)
    positions = jnp.arange(SEQ_LEN, dtype=jnp.int32)
    causal = positions[:, None] >= positions[None, :]

    def one_head(operands):
        query_one, key_one, value_one = operands
        scores = jnp.dot(query_one, key_one.T, preferred_element_type=jnp.float32) * score_scale
        row_max = lax.optimization_barrier(jnp.max(jnp.where(causal, scores, -jnp.inf), axis=1, keepdims=True))
        weights = jnp.where(causal, jnp.exp(scores - row_max), 0.0)
        totals = lax.optimization_barrier(jnp.sum(weights, axis=1, keepdims=True))
        return jnp.dot(weights.astype(jnp.bfloat16), value_one, preferred_element_type=jnp.float32) / totals
    attended = lax.map(one_head, (query_heads, key_heads, value_heads))
    attended = attended.transpose(1, 0, 2).reshape(SEQ_LEN, D)
    combined = (hyena_out + attended).astype(jnp.bfloat16)
    mixed = jnp.dot(combined, out_weight, preferred_element_type=jnp.float32).astype(jnp.bfloat16)
    return mixed.reshape(2 * N_CTX, CH, D)[stretch_slot].reshape(SEQ_LEN, D)
```

```python
import math

import jax
import jax.numpy as jnp
from jax import lax
from jax.experimental import pallas as pl
from jax.experimental.pallas import tpu as pltpu
from jax.sharding import PartitionSpec as P

HD = 128
CH = 64
NY = 4
NZ = 4
SPLIT = 384
F32 = jnp.float32
BF16 = jnp.bfloat16
NEG = -1e30

ORD_P = (0, 3, 1, 2)
ORD_Q = (0, 1, 3, 2)


def local_kernel(conv_ref, val_ref, rate_ref, res_ref, skip_ref, base_ref, st_ref, p_scr, h_scr):
    modes = rate_ref.shape[0]
    prod = conv_ref[...].astype(F32) * val_ref[...].astype(F32)
    p_scr[...] = prod
    rate = rate_ref[...]
    rows = lax.broadcasted_iota(jnp.int32, (8, HD), 0)
    rows_f = rows.astype(F32)
    step8 = jnp.exp(-8.0 * rate)
    taps = [jnp.zeros((8, HD), F32) for _ in range(8)]
    for n in range(modes):
        term = res_ref[n : n + 1, :] * jnp.exp(-rate[n : n + 1, :] * rows_f)
        factor = jnp.broadcast_to(step8[n : n + 1, :], (8, HD))
        for k in range(8):
            taps[k] = taps[k] + term
            if k < 7:
                term = term * factor
    for s in range(8):
        previous = jnp.zeros((8, HD), F32)
        for k in range(8):
            if s == 0:
                shifted = taps[k]
            else:
                rolled = pltpu.roll(taps[k], s, 0)
                shifted = jnp.where(rows < s, previous, rolled)
                previous = rolled
            h_scr[s * 64 + 8 * k : s * 64 + 8 * k + 8, :] = shifted
    skip = skip_ref[...]
    acc = [[jnp.zeros((8, HD), F32) for _ in range(8)] for _ in range(2)]
    decay = jnp.exp(-rate)
    states = [jnp.zeros((modes, HD), F32) for _ in range(2)]
    for j in range(CH):
        jt, s = j // 8, j % 8
        inputs = [p_scr[m * CH + j : m * CH + j + 1, :] for m in range(2)]
        wide = [jnp.broadcast_to(v, (8, HD)) for v in inputs]
        for it in range(jt, 8):
            tap = h_scr[s * 64 + 8 * (it - jt) : s * 64 + 8 * (it - jt) + 8, :]
            for m in range(2):
                acc[m][it] = acc[m][it] + tap * wide[m]
        for m in range(2):
            states[m] = decay * states[m] + inputs[m]
    for m in range(2):
        st_ref[m] = states[m].astype(BF16)
        for it in range(8):
            at = m * CH + 8 * it
            base_ref[at : at + 8, :] = acc[m][it] + skip * p_scr[at : at + 8, :]


def local_stage(conv_in, value_in, rate, residue, skip):
    rows, channels = conv_in.shape
    modes = rate.shape[0]
    heads = channels // HD
    return pl.pallas_call(
        local_kernel,
        grid=(heads,),
        in_specs=[
            pl.BlockSpec((rows, HD), lambda h: (0, h)),
            pl.BlockSpec((rows, HD), lambda h: (0, h)),
            pl.BlockSpec((modes, HD), lambda h: (0, h)),
            pl.BlockSpec((modes, HD), lambda h: (0, h)),
            pl.BlockSpec((1, HD), lambda h: (0, h)),
        ],
        out_specs=[
            pl.BlockSpec((rows, HD), lambda h: (0, h)),
            pl.BlockSpec((2, modes, HD), lambda h: (0, 0, h)),
        ],
        out_shape=[
            jax.ShapeDtypeStruct((rows, channels), F32),
            jax.ShapeDtypeStruct((2, modes, channels), BF16),
        ],
        scratch_shapes=[pltpu.VMEM((rows, HD), F32), pltpu.VMEM((512, HD), F32)],
        name="local_conv",
    )(conv_in, value_in, rate, residue, skip)


def mix_kernel(
    slot_ref, q_ref, k0, k1, k2, k3, v0, v1, v2, v3, s0, s1, s2, s3, rate_ref, res_ref, gate_ref, base_ref, w_ref,
    send_a, send_b, send_c, send_d, keep_a, keep_b, keep_c, keep_d,
    w_scr, bias_scr, comb_scr, sems,
):
    rows, channels = q_ref.shape
    modes = rate_ref.shape[0]
    heads = channels // HD
    ctx = lax.axis_index("ctx")
    head = lax.axis_index("head")
    my_y, my_z = head // NZ, head % NZ
    order = [(a, b) for a in (2, 1, 3, 0) for b in (2, 1, 3, 0)]
    copies = []
    for i, (a, b) in enumerate(order):
        chunk = (my_y ^ a) * NZ + (my_z ^ b)
        copies.append(
            pltpu.make_async_copy(w_ref.at[:, pl.ds(chunk * channels, channels)], w_scr.at[i], sems.at[i])
        )
        copies[-1].start()
    masks = (0, 1, 3, 2)
    key_st = [slot_ref[2 * (ctx ^ m) + s] for m in masks for s in range(2)]
    my_st = key_st[:2]
    col = lax.broadcasted_iota(jnp.int32, (rows, HD), 1)
    row = lax.broadcasted_iota(jnp.int32, (rows, HD), 0)
    q_pos = jnp.where(row < CH, my_st[0] * CH + row, my_st[1] * CH + row - CH)
    for r in range(4):
        k_pos = jnp.where(col < CH, key_st[2 * r] * CH + col, key_st[2 * r + 1] * CH + col - CH)
        bias_scr[r] = jnp.where(k_pos <= q_pos, 0.0, NEG)
    rows_f = (lax.broadcasted_iota(jnp.int32, (8, HD), 0) + 1).astype(F32)
    scale = 1.0 / math.sqrt(HD)
    for h in range(heads):
        at = slice(h * HD, (h + 1) * HD)
        rate = rate_ref[:, at]
        residue = res_ref[:, at]
        pieces = [s[i, :, at].astype(F32) for s in (s0, s1, s2, s3) for i in range(2)]
        entry = []
        for m in range(2):
            total = jnp.zeros((modes, HD), F32)
            for piece, stretch in zip(pieces, key_st):
                gap = my_st[m] - 1 - stretch
                span = (CH * jnp.maximum(gap, 0)).astype(F32)
                weight = jnp.where(gap >= 0, 1.0, 0.0)
                total = total + (weight * jnp.exp(-rate * span)) * piece
            entry.append(residue * total)
        step8 = jnp.exp(-8.0 * rate)
        carry = [[jnp.zeros((8, HD), F32) for _ in range(8)] for _ in range(2)]
        for n in range(modes):
            term = jnp.exp(-rate[n : n + 1, :] * rows_f)
            factor = jnp.broadcast_to(step8[n : n + 1, :], (8, HD))
            wide = [jnp.broadcast_to(entry[m][n : n + 1, :], (8, HD)) for m in range(2)]
            for k in range(8):
                for m in range(2):
                    carry[m][k] = carry[m][k] + term * wide[m]
                if k < 7:
                    term = term * factor
        carried = jnp.concatenate([carry[m][k] for m in range(2) for k in range(8)], axis=0)
        hyena = gate_ref[:, at].astype(F32) * (base_ref[:, at] + carried)
        query = q_ref[:, at]
        scores = [
            lax.dot_general(query, k[:, at], (((1,), (1,)), ((), ())), preferred_element_type=F32) * scale
            + bias_scr[r]
            for r, k in enumerate((k0, k1, k2, k3))
        ]
        peak = jnp.maximum(jnp.maximum(scores[0], scores[1]), jnp.maximum(scores[2], scores[3]))
        peak = jnp.max(peak, axis=1, keepdims=True)
        probs = [jnp.exp(s - peak) for s in scores]
        total = jnp.sum((probs[0] + probs[1]) + (probs[2] + probs[3]), axis=1, keepdims=True)
        mixed = None
        for p, v in zip(probs, (v0, v1, v2, v3)):
            part = jnp.dot(p.astype(BF16), v[:, at], preferred_element_type=F32)
            mixed = part if mixed is None else mixed + part
        comb_scr[:, at] = (hyena + mixed / total).astype(BF16)
    comb = comb_scr[...]
    for i, (a, b) in enumerate(order):
        copies[i].wait()
        part = jnp.dot(comb, w_scr[i], preferred_element_type=F32)
        for which, (send, keep) in enumerate(((send_a, keep_a), (send_b, keep_b), (send_c, keep_c), (send_d, keep_d))):
            lead, other = (a, b) if which < 2 else (b, a)
            orders = ORD_P if which % 2 == 0 else ORD_Q
            x = orders.index(lead)
            y = orders.index(other)
            block = part[CH * (which % 2) : CH * (which % 2) + CH, :]
            block = block[:, :SPLIT] if which < 2 else block[:, SPLIT:]
            if x < 2:
                keep[x, y] = block.astype(keep.dtype)
            else:
                send[x - 2, y] = block.astype(BF16)


def mix_stage(slots, query, keys, values, states, rate, residue, gate, base, weight):
    rows, channels = query.shape
    wide, thin = (2, 4, CH, SPLIT), (2, 4, CH, channels - SPLIT)
    vmem = pl.BlockSpec(memory_space=pltpu.VMEM)
    shapes = [wide, wide, thin, thin]
    return pl.pallas_call(
        mix_kernel,
        in_specs=[pl.BlockSpec(memory_space=pltpu.SMEM)] + [vmem] * 17 + [pl.BlockSpec(memory_space=pl.ANY)],
        out_specs=[vmem] * 8,
        out_shape=[jax.ShapeDtypeStruct(s, BF16) for s in shapes] + [jax.ShapeDtypeStruct(s, F32) for s in shapes],
        scratch_shapes=[
            pltpu.VMEM((NY * NZ, channels, channels), BF16),
            pltpu.VMEM((4, rows, HD), F32),
            pltpu.VMEM((rows, channels), BF16),
            pltpu.SemaphoreType.DMA((NY * NZ,)),
        ],
        name="mix_project",
    )(slots, query, *keys, *values, *states, rate, residue, gate, base, weight)


def swap(value, axis, mask):
    if axis == "ctx":
        pairs = [(i, i ^ mask) for i in range(4)]
        return lax.ppermute(value, "ctx", pairs)
    if axis == "y":
        pairs = [(y * NZ + z, (y ^ mask) * NZ + z) for y in range(NY) for z in range(NZ)]
    else:
        pairs = [(y * NZ + z, y * NZ + (z ^ mask)) for y in range(NY) for z in range(NZ)]
    return lax.ppermute(value, "head", pairs)


def body(
    stretch_slot, gate_in, conv_in, value_in, modal_rate, modal_residue, skip_gain, query_proj, key_proj, value_proj,
    out_weight,
):
    k1 = swap(key_proj, "ctx", 1)
    v3 = swap(value_proj, "ctx", 3)
    k3 = swap(key_proj, "ctx", 3)
    v1 = swap(value_proj, "ctx", 1)
    base, state = local_stage(conv_in, value_in, modal_rate, modal_residue, skip_gain[None, :])
    s1 = swap(state, "ctx", 1)
    s3 = swap(state, "ctx", 3)
    k2 = swap(k1, "ctx", 3)
    v2 = swap(v3, "ctx", 1)
    s2 = swap(s1, "ctx", 3)
    outs = mix_stage(
        stretch_slot, query_proj, (key_proj, k1, k3, k2), (value_proj, v1, v3, v2), (state, s1, s3, s2),
        modal_rate, modal_residue, gate_in, base, out_weight,
    )
    sends, keeps = outs[:4], outs[4:]
    plans = (
        (("y", 1), ("y", 3), ("z", 1), ("z", 3)),
        (("y", 3), ("y", 1), ("z", 3), ("z", 1)),
        (("z", 1), ("z", 3), ("y", 1), ("y", 3)),
        (("z", 3), ("z", 1), ("y", 3), ("y", 1)),
    )
    sends, keeps = list(sends), list(keeps)
    got = [swap(sends[i], *plans[i][0]) for i in range(4)]
    for i in range(4):
        sends[i] = (keeps[i][1] + got[i][1].astype(F32)).astype(BF16)
        keeps[i] = keeps[i][0] + got[i][0].astype(F32)
    got = [swap(sends[i], *plans[i][1]) for i in range(4)]
    for i in range(4):
        sends[i] = (keeps[i][2:] + got[i][2:].astype(F32)).astype(BF16)
        keeps[i] = keeps[i][:2] + got[i][:2].astype(F32)
    got = [swap(sends[i], *plans[i][2]) for i in range(4)]
    for i in range(4):
        sends[i] = (keeps[i][1] + got[i][1].astype(F32)).astype(BF16)
        keeps[i] = keeps[i][0] + got[i][0].astype(F32)
    got = [swap(sends[i], *plans[i][3]) for i in range(4)]
    parts = [(keeps[i] + got[i].astype(F32)).astype(BF16) for i in range(4)]
    return jnp.concatenate(
        [jnp.concatenate([parts[0], parts[2]], axis=1), jnp.concatenate([parts[1], parts[3]], axis=1)], axis=0
    )


def solution(mesh):
    return jax.shard_map(
        body,
        mesh=mesh,
        in_specs=(
            P("seq"),
            P(("seq", "ctx"), "head"),
            P(("seq", "ctx"), "head"),
            P(("seq", "ctx"), "head"),
            P("seq", "head"),
            P("seq", "head"),
            P(("seq", "head")),
            P(("seq", "ctx"), "head"),
            P(("seq", "ctx"), "head"),
            P(("seq", "ctx"), "head"),
            P(("seq", "head"), None),
        ),
        out_specs=P(("seq", "ctx"), "head"),
        check_vma=False,
    )
```

```python
import math

import jax
import jax.numpy as jnp
from jax import lax
from jax.experimental import pallas as pl
from jax.experimental.pallas import tpu as pltpu
from jax.sharding import PartitionSpec as P

HD = 128
CH = 64
NY = 4
NZ = 4
F32 = jnp.float32
BF16 = jnp.bfloat16
NEG = -1e30

ORD_P = (0, 3, 1, 2)
ORD_Q = (0, 1, 3, 2)


def pack_kernel(conv_hbm, val_hbm, rate_hbm, key_hbm, value_hbm, out_ref, p_ref, conv_scr, val_scr, rate_scr, sems):
    rows, channels = conv_scr.shape
    modes = rate_scr.shape[0]
    sources = (conv_hbm, val_hbm, rate_hbm, key_hbm, value_hbm)
    targets = (conv_scr, val_scr, rate_scr, out_ref.at[0, pl.ds(0, rows), :], out_ref.at[1, pl.ds(0, rows), :])
    copies = [pltpu.make_async_copy(s, t, sems.at[i]) for i, (s, t) in enumerate(zip(sources, targets))]
    for copy in copies:
        copy.start()
    for copy in copies[:3]:
        copy.wait()
    p_ref[...] = conv_scr[...].astype(F32) * val_scr[...].astype(F32)
    decay = jnp.exp(-rate_scr[...])
    states = [jnp.zeros((modes, channels), F32) for _ in range(2)]
    for j in range(CH):
        for m in range(2):
            states[m] = decay * states[m] + p_ref[m * CH + j : m * CH + j + 1, :]
    for m in range(2):
        out_ref[m, rows:, :] = states[m].astype(BF16)
    for copy in copies[3:]:
        copy.wait()


def pack_stage(conv_in, value_in, rate, keys, values):
    rows, channels = conv_in.shape
    modes = rate.shape[0]
    vmem = pl.BlockSpec(memory_space=pltpu.VMEM)
    hbm = pl.BlockSpec(memory_space=pltpu.HBM)
    return pl.pallas_call(
        pack_kernel,
        in_specs=[hbm] * 5,
        out_specs=[vmem, vmem],
        out_shape=[
            jax.ShapeDtypeStruct((2, rows + modes, channels), BF16),
            jax.ShapeDtypeStruct((rows, channels), F32),
        ],
        scratch_shapes=[
            pltpu.VMEM((rows, channels), BF16),
            pltpu.VMEM((rows, channels), BF16),
            pltpu.VMEM((modes, channels), F32),
            pltpu.SemaphoreType.DMA((5,)),
        ],
        compiler_params=pltpu.CompilerParams(vmem_limit_bytes=4 << 20),
        name="pack_states",
    )(conv_in, value_in, rate, keys, values)


CHUNKS = [(a, b) for a in (2, 1, 3, 0) for b in (2, 1, 3, 0)]


def local_kernel(
    p_ref, slot_hbm, rate_hbm, res_hbm, skip_hbm, query_hbm, gate_hbm, weight_hbm,
    base_ref, bias_ref, pull_ref, rate_ref, res_ref, query_ref, gate_ref, weight_ref,
    slot_ref, skip_ref, h_scr, sems, wsems,
):
    rows, channels = p_ref.shape
    modes = rate_ref.shape[0]
    heads = channels // HD
    ctx = lax.axis_index("ctx")
    head = lax.axis_index("head")
    my_y, my_z = head // NZ, head % NZ
    sources = (rate_hbm, res_hbm, skip_hbm, slot_hbm, query_hbm, gate_hbm)
    targets = (rate_ref, res_ref, skip_ref, slot_ref, query_ref, gate_ref)
    copies = [pltpu.make_async_copy(s, t, sems.at[i]) for i, (s, t) in enumerate(zip(sources, targets))]
    for copy in copies:
        copy.start()
    loads = []
    for i, (a, b) in enumerate(CHUNKS):
        chunk = (my_y ^ a) * NZ + (my_z ^ b)
        loads.append(
            pltpu.make_async_copy(weight_hbm.at[:, pl.ds(chunk * channels, channels)], weight_ref.at[i], wsems.at[i])
        )
        loads[-1].start()
    for copy in copies:
        copy.wait()
    index = lax.broadcasted_iota(jnp.int32, (8, HD), 0)
    index_f = index.astype(F32)

    def one_head(h, carry):
        at = pl.ds(pl.multiple_of(h * HD, HD), HD)
        step8 = jnp.exp(-8.0 * rate_ref[:, at])
        taps = [jnp.zeros((8, HD), F32) for _ in range(8)]
        for n in range(modes):
            term = res_ref[n : n + 1, at] * jnp.exp(-rate_ref[n : n + 1, at] * index_f)
            factor = jnp.broadcast_to(step8[n : n + 1, :], (8, HD))
            for k in range(8):
                taps[k] = taps[k] + term
                if k < 7:
                    term = term * factor
        for s in range(8):
            previous = jnp.zeros((8, HD), F32)
            for k in range(8):
                if s == 0:
                    shifted = taps[k]
                else:
                    rolled = pltpu.roll(taps[k], s, 0)
                    shifted = jnp.where(index < s, previous, rolled)
                    previous = rolled
                h_scr[s * 64 + 8 * k : s * 64 + 8 * k + 8, :] = shifted
        skip = skip_ref[:, at]
        acc = [[jnp.zeros((8, HD), F32) for _ in range(8)] for _ in range(2)]
        for j in range(CH):
            jt, s = j // 8, j % 8
            wide = [jnp.broadcast_to(p_ref[m * CH + j : m * CH + j + 1, at], (8, HD)) for m in range(2)]
            for it in range(jt, 8):
                tap = h_scr[s * 64 + 8 * (it - jt) : s * 64 + 8 * (it - jt) + 8, :]
                for m in range(2):
                    acc[m][it] = acc[m][it] + tap * wide[m]
        for m in range(2):
            for it in range(8):
                row = m * CH + 8 * it
                base_ref[row : row + 8, at] = acc[m][it] + skip * p_ref[row : row + 8, at]
        return carry

    lax.fori_loop(0, heads, one_head, 0)
    key_st = [slot_ref[2 * (ctx ^ m) + s] for m in (0, 1, 3, 2) for s in range(2)]
    my_st = key_st[:2]
    col = lax.broadcasted_iota(jnp.int32, (rows, HD), 1)
    row = lax.broadcasted_iota(jnp.int32, (rows, HD), 0)
    q_pos = jnp.where(row < CH, my_st[0] * CH + row, my_st[1] * CH + row - CH)
    for r in range(4):
        k_pos = jnp.where(col < CH, key_st[2 * r] * CH + col, key_st[2 * r + 1] * CH + col - CH)
        bias_ref[r] = jnp.where(k_pos <= q_pos, 0.0, NEG)
    for m in range(2):
        for i, stretch in enumerate(key_st):
            gap = my_st[m] - 1 - stretch
            span = (CH * jnp.maximum(gap, 0)).astype(F32)
            pull_ref[m, i] = jnp.where(gap >= 0, 1.0, 0.0) * (res_ref[...] * jnp.exp(-rate_ref[...] * span))
    for load in loads:
        load.wait()


def local_stage(product, slots, rate, residue, skip, query, gate, weight):
    rows, channels = product.shape
    modes = rate.shape[0]
    vmem = pl.BlockSpec(memory_space=pltpu.VMEM)
    hbm = pl.BlockSpec(memory_space=pltpu.HBM)
    return pl.pallas_call(
        local_kernel,
        in_specs=[vmem] + [hbm] * 7,
        out_specs=[vmem] * 8,
        out_shape=[
            jax.ShapeDtypeStruct((rows, channels), F32),
            jax.ShapeDtypeStruct((4, rows, HD), F32),
            jax.ShapeDtypeStruct((2, 8, modes, channels), F32),
            jax.ShapeDtypeStruct(rate.shape, F32),
            jax.ShapeDtypeStruct(residue.shape, F32),
            jax.ShapeDtypeStruct(query.shape, BF16),
            jax.ShapeDtypeStruct(gate.shape, BF16),
            jax.ShapeDtypeStruct((NY * NZ, channels, channels), BF16),
        ],
        scratch_shapes=[
            pltpu.SMEM(slots.shape, jnp.int32),
            pltpu.VMEM(skip.shape, F32),
            pltpu.VMEM((512, HD), F32),
            pltpu.SemaphoreType.DMA((6,)),
            pltpu.SemaphoreType.DMA((NY * NZ,)),
        ],
        compiler_params=pltpu.CompilerParams(vmem_limit_bytes=16 << 20),
        name="local_conv",
    )(product, slots, rate, residue, skip, query, gate, weight)


def mix_kernel(
    own_ref, one_ref, three_ref, k2_ref, v2_ref, base_ref, bias_ref, pull_ref, rate_ref, query_ref, gate_ref, w_ref,
    send_p, send_q, keep_p, keep_q, comb_scr,
):
    rows, channels = query_ref.shape
    modes = rate_ref.shape[0]
    heads = channels // HD
    first = (own_ref.at[0], one_ref.at[0], three_ref.at[0], k2_ref)
    second = (own_ref.at[1], one_ref.at[1], three_ref.at[1], v2_ref)
    rows_f = (lax.broadcasted_iota(jnp.int32, (8, HD), 0) + 1).astype(F32)
    scale = 1.0 / math.sqrt(HD)
    for h in range(heads):
        at = slice(h * HD, (h + 1) * HD)
        rate = rate_ref[:, at]
        pieces = [s[rows:, at].astype(F32) for pair in zip(first, second) for s in pair]
        entry = []
        for m in range(2):
            total = pull_ref[m, 0, :, at] * pieces[0]
            for i in range(1, 8):
                total = total + pull_ref[m, i, :, at] * pieces[i]
            entry.append(total)
        step8 = jnp.exp(-8.0 * rate)
        carry = [[jnp.zeros((8, HD), F32) for _ in range(8)] for _ in range(2)]
        for n in range(modes):
            term = jnp.exp(-rate[n : n + 1, :] * rows_f)
            factor = jnp.broadcast_to(step8[n : n + 1, :], (8, HD))
            wide = [jnp.broadcast_to(entry[m][n : n + 1, :], (8, HD)) for m in range(2)]
            for k in range(8):
                for m in range(2):
                    carry[m][k] = carry[m][k] + term * wide[m]
                if k < 7:
                    term = term * factor
        carried = jnp.concatenate([carry[m][k] for m in range(2) for k in range(8)], axis=0)
        hyena = gate_ref[:, at].astype(F32) * (base_ref[:, at] + carried)
        query = query_ref[:, at]
        scores = [
            lax.dot_general(query, k[:rows, at], (((1,), (1,)), ((), ())), preferred_element_type=F32) * scale
            + bias_ref[r]
            for r, k in enumerate(first)
        ]
        peak = jnp.maximum(jnp.maximum(scores[0], scores[1]), jnp.maximum(scores[2], scores[3]))
        peak = jnp.max(peak, axis=1, keepdims=True)
        probs = [jnp.exp(s - peak) for s in scores]
        total = jnp.sum((probs[0] + probs[1]) + (probs[2] + probs[3]), axis=1, keepdims=True)
        mixed = None
        for p, v in zip(probs, second):
            part = jnp.dot(p.astype(BF16), v[:rows, at], preferred_element_type=F32)
            mixed = part if mixed is None else mixed + part
        comb_scr[:, at] = (hyena + mixed / total).astype(BF16)
    comb = comb_scr[...]
    for i, (a, b) in enumerate(CHUNKS):
        part = jnp.dot(comb, w_ref[i], preferred_element_type=F32)
        for which, (send, keep) in enumerate(((send_p, keep_p), (send_q, keep_q))):
            orders = ORD_P if which == 0 else ORD_Q
            x = orders.index(a)
            y = orders.index(b)
            block = part[CH * which : CH * which + CH, :].astype(BF16)
            if x < 2:
                keep[x, y] = block
            else:
                send[x - 2, y] = block


def mix_stage(own, one, three, k2, v2, base, bias, pull, rate, query, gate, weight):
    rows, channels = query.shape
    vmem = pl.BlockSpec(memory_space=pltpu.VMEM)
    return pl.pallas_call(
        mix_kernel,
        in_specs=[vmem] * 12,
        out_specs=[vmem] * 4,
        out_shape=[jax.ShapeDtypeStruct((2, 4, CH, channels), BF16)] * 4,
        scratch_shapes=[pltpu.VMEM((rows, channels), BF16)],
        compiler_params=pltpu.CompilerParams(vmem_limit_bytes=20 << 20),
        name="mix_project",
    )(own, one, three, k2, v2, base, bias, pull, rate, query, gate, weight)


def swap(value, axis, mask):
    if axis == "ctx":
        pairs = [(i, i ^ mask) for i in range(4)]
        return lax.ppermute(value, "ctx", pairs)
    if axis == "y":
        pairs = [(y * NZ + z, (y ^ mask) * NZ + z) for y in range(NY) for z in range(NZ)]
    else:
        pairs = [(y * NZ + z, y * NZ + (z ^ mask)) for y in range(NY) for z in range(NZ)]
    return lax.ppermute(value, "head", pairs)


def body(
    stretch_slot, gate_in, conv_in, value_in, modal_rate, modal_residue, skip_gain, query_proj, key_proj, value_proj,
    out_weight,
):
    conv_in, value_in, key_proj, value_proj, query_proj, gate_in, out_weight, modal_rate, modal_residue = (
        pltpu.with_memory_space_constraint(x, pltpu.HBM)
        for x in (
            conv_in, value_in, key_proj, value_proj, query_proj, gate_in, out_weight, modal_rate, modal_residue
        )
    )
    slots = pltpu.with_memory_space_constraint(stretch_slot, pltpu.HBM)
    skip = pltpu.with_memory_space_constraint(skip_gain[None, :], pltpu.HBM)
    own, product = pack_stage(conv_in, value_in, modal_rate, key_proj, value_proj)
    one = swap(own, "ctx", 1)
    three = swap(own, "ctx", 3)
    base, bias, pull, rate, _, query, gate, weight = local_stage(
        product, slots, modal_rate, modal_residue, skip, query_proj, gate_in, out_weight
    )
    one, three, base = lax.optimization_barrier((one, three, base))
    k2 = swap(one[0], "ctx", 3)
    v2 = swap(three[1], "ctx", 1)
    send_p, send_q, keep_p, keep_q = mix_stage(own, one, three, k2, v2, base, bias, pull, rate, query, gate, weight)

    def total(*terms):
        result = terms[0].astype(F32)
        for term in terms[1:]:
            result = result + term.astype(F32)
        return result.astype(BF16)

    keeps = (keep_p, keep_q)
    plans = ((("y", 1), ("y", 3), ("z", 1), ("z", 3)), (("y", 3), ("y", 1), ("z", 3), ("z", 1)))
    first = [swap(send, *plan[0]) for send, plan in zip((send_p, send_q), plans)]
    second = [swap(total(k[1], a[1]), *plan[1]) for k, a, plan in zip(keeps, first, plans)]
    third = [swap(total(k[0, 2:], a[0, 2:], b[2:]), *plan[2]) for k, a, b, plan in zip(keeps, first, second, plans)]
    fourth = [
        swap(total(k[0, 1], a[0, 1], b[1], c[1]), *plan[3])
        for k, a, b, c, plan in zip(keeps, first, second, third, plans)
    ]
    parts = [
        total(k[0, 0], a[0, 0], b[0], c[0], d) for k, a, b, c, d in zip(keeps, first, second, third, fourth)
    ]
    return jnp.concatenate(parts, axis=0)


def solution(mesh):
    return jax.shard_map(
        body,
        mesh=mesh,
        in_specs=(
            P("seq"),
            P(("seq", "ctx"), "head"),
            P(("seq", "ctx"), "head"),
            P(("seq", "ctx"), "head"),
            P("seq", "head"),
            P("seq", "head"),
            P(("seq", "head")),
            P(("seq", "ctx"), "head"),
            P(("seq", "ctx"), "head"),
            P(("seq", "ctx"), "head"),
            P(("seq", "head"), None),
        ),
        out_specs=P(("seq", "ctx"), "head"),
        check_vma=False,
    )
```

```python
import math

import jax
import jax.numpy as jnp
from jax import lax
from jax.experimental import pallas as pl
from jax.experimental.pallas import tpu as pltpu
from jax.sharding import PartitionSpec as P


HD = 128
CH = 64
NY = 4
NZ = 4
F32 = jnp.float32
BF16 = jnp.bfloat16
NEG = -1e30

ORD_P = (0, 3, 1, 2)
ORD_Q = (0, 1, 3, 2)


def pack_kernel(
    conv_hbm, val_hbm, rate_hbm, key_hbm, value_hbm, res_hbm, skip_hbm,
    a_ref, b_ref, p_ref, rate_ref, res_ref, skip_ref, conv_scr, val_scr, sems,
):
    rows, channels = conv_scr.shape
    modes = rate_ref.shape[0]
    sources = (conv_hbm, val_hbm, rate_hbm, key_hbm, value_hbm, res_hbm, skip_hbm)
    targets = (
        conv_scr, val_scr, rate_ref, a_ref.at[pl.ds(0, rows), :], b_ref.at[pl.ds(0, rows), :], res_ref, skip_ref
    )
    copies = [pltpu.make_async_copy(s, t, sems.at[i]) for i, (s, t) in enumerate(zip(sources, targets))]
    for copy in copies:
        copy.start()
    for copy in copies[:3]:
        copy.wait()
    p_ref[...] = conv_scr[...].astype(F32) * val_scr[...].astype(F32)
    decay = jnp.exp(-rate_ref[...])
    states = [jnp.zeros((modes, channels), F32) for _ in range(2)]
    for j in range(CH):
        for m in range(2):
            states[m] = decay * states[m] + p_ref[m * CH + j : m * CH + j + 1, :]
    a_ref[rows:, :] = states[0].astype(BF16)
    b_ref[rows:, :] = states[1].astype(BF16)
    for copy in copies[3:]:
        copy.wait()


def pack_stage(conv_in, value_in, rate, keys, values, residue, skip):
    rows, channels = conv_in.shape
    modes = rate.shape[0]
    vmem = pl.BlockSpec(memory_space=pltpu.VMEM)
    hbm = pl.BlockSpec(memory_space=pltpu.HBM)
    return pl.pallas_call(
        pack_kernel,
        in_specs=[hbm] * 7,
        out_specs=[vmem] * 6,
        out_shape=[
            jax.ShapeDtypeStruct((rows + modes, channels), BF16),
            jax.ShapeDtypeStruct((rows + modes, channels), BF16),
            jax.ShapeDtypeStruct((rows, channels), F32),
            jax.ShapeDtypeStruct(rate.shape, F32),
            jax.ShapeDtypeStruct(residue.shape, F32),
            jax.ShapeDtypeStruct(skip.shape, F32),
        ],
        scratch_shapes=[
            pltpu.VMEM((rows, channels), BF16),
            pltpu.VMEM((rows, channels), BF16),
            pltpu.SemaphoreType.DMA((7,)),
        ],
        compiler_params=pltpu.CompilerParams(vmem_limit_bytes=4 << 20),
        name="pack_states",
    )(conv_in, value_in, rate, keys, values, residue, skip)


BLOCKS = 4


def weight_loads(weight_hbm, weight_ref, sems, start):
    block = weight_ref.shape[0] // BLOCKS
    loads = [
        pltpu.make_async_copy(
            weight_hbm.at[pl.ds(start + i * block, block), :], weight_ref.at[pl.ds(i * block, block), :], sems.at[i]
        )
        for i in range(BLOCKS)
    ]
    for load in loads:
        load.start()
    return loads


CHUNKS = [(a, b) for a in (2, 1, 3, 0) for b in (2, 1, 3, 0)]


def local_kernel(p_ref, rate_ref, res_ref, skip_ref, weight_hbm, base_ref, weight_ref, h_scr, wsems):
    channels = p_ref.shape[1]
    modes = rate_ref.shape[0]
    heads = channels // HD
    loads = weight_loads(weight_hbm, weight_ref, wsems, 0)
    index = lax.broadcasted_iota(jnp.int32, (8, HD), 0)
    index_f = index.astype(F32)

    for h in range(heads):
        at = slice(h * HD, (h + 1) * HD)
        step8 = jnp.exp(-8.0 * rate_ref[:, at])
        taps = [jnp.zeros((8, HD), F32) for _ in range(8)]
        for n in range(modes):
            term = res_ref[n : n + 1, at] * jnp.exp(-rate_ref[n : n + 1, at] * index_f)
            factor = jnp.broadcast_to(step8[n : n + 1, :], (8, HD))
            for k in range(8):
                taps[k] = taps[k] + term
                if k < 7:
                    term = term * factor
        for s in range(8):
            previous = jnp.zeros((8, HD), F32)
            for k in range(8):
                if s == 0:
                    shifted = taps[k]
                else:
                    rolled = pltpu.roll(taps[k], s, 0)
                    shifted = jnp.where(index < s, previous, rolled)
                    previous = rolled
                h_scr[s * 64 + 8 * k : s * 64 + 8 * k + 8, :] = shifted
        skip = skip_ref[:, at]
        acc = [[jnp.zeros((8, HD), F32) for _ in range(8)] for _ in range(2)]
        for j in range(CH):
            jt, s = j // 8, j % 8
            wide = [jnp.broadcast_to(p_ref[m * CH + j : m * CH + j + 1, at], (8, HD)) for m in range(2)]
            for it in range(jt, 8):
                tap = h_scr[s * 64 + 8 * (it - jt) : s * 64 + 8 * (it - jt) + 8, :]
                for m in range(2):
                    acc[m][it] = acc[m][it] + tap * wide[m]
        for m in range(2):
            for it in range(8):
                row = m * CH + 8 * it
                base_ref[row : row + 8, at] = acc[m][it] + skip * p_ref[row : row + 8, at]
    for load in loads:
        load.wait()


def local_stage(product, rate, residue, skip, weight):
    vmem = pl.BlockSpec(memory_space=pltpu.VMEM)
    return pl.pallas_call(
        local_kernel,
        in_specs=[vmem] * 4 + [pl.BlockSpec(memory_space=pltpu.HBM)],
        out_specs=[vmem] * 2,
        out_shape=[
            jax.ShapeDtypeStruct(product.shape, F32),
            jax.ShapeDtypeStruct((weight.shape[0] // 2, weight.shape[1]), BF16),
        ],
        scratch_shapes=[pltpu.VMEM((512, HD), F32), pltpu.SemaphoreType.DMA((BLOCKS,))],
        compiler_params=pltpu.CompilerParams(vmem_limit_bytes=8 << 20),
        name="local_conv",
    )(product, rate, residue, skip, weight)


def fetch_kernel(
    rate_ref, res_ref, slot_hbm, query_hbm, gate_hbm, weight_hbm,
    bias_ref, pull_ref, query_ref, gate_ref, weight_ref, slot_ref, sems, wsems,
):
    rows = query_ref.shape[0]
    ctx = lax.axis_index("ctx")
    sources = (slot_hbm, query_hbm, gate_hbm)
    targets = (slot_ref, query_ref, gate_ref)
    copies = [pltpu.make_async_copy(s, t, sems.at[i]) for i, (s, t) in enumerate(zip(sources, targets))]
    for copy in copies:
        copy.start()
    loads = weight_loads(weight_hbm, weight_ref, wsems, weight_ref.shape[0])
    for copy in copies:
        copy.wait()
    key_st = [slot_ref[2 * (ctx ^ m) + s] for m in (0, 1, 3, 2) for s in range(2)]
    my_st = key_st[:2]
    col = lax.broadcasted_iota(jnp.int32, (rows, HD), 1)
    row = lax.broadcasted_iota(jnp.int32, (rows, HD), 0)
    q_pos = jnp.where(row < CH, my_st[0] * CH + row, my_st[1] * CH + row - CH)
    for r in range(4):
        k_pos = jnp.where(col < CH, key_st[2 * r] * CH + col, key_st[2 * r + 1] * CH + col - CH)
        bias_ref[r] = jnp.where(k_pos <= q_pos, 0.0, NEG)
    for m in range(2):
        for i, stretch in enumerate(key_st):
            gap = my_st[m] - 1 - stretch
            span = (CH * jnp.maximum(gap, 0)).astype(F32)
            pull_ref[m, i] = jnp.where(gap >= 0, 1.0, 0.0) * (res_ref[...] * jnp.exp(-rate_ref[...] * span))
    for load in loads:
        load.wait()


def fetch_stage(rate, residue, slots, query, gate, weight):
    rows, channels = query.shape
    vmem = pl.BlockSpec(memory_space=pltpu.VMEM)
    hbm = pl.BlockSpec(memory_space=pltpu.HBM)
    return pl.pallas_call(
        fetch_kernel,
        in_specs=[vmem] * 2 + [hbm] * 4,
        out_specs=[vmem] * 5,
        out_shape=[
            jax.ShapeDtypeStruct((4, rows, HD), F32),
            jax.ShapeDtypeStruct((2, 8) + rate.shape, F32),
            jax.ShapeDtypeStruct(query.shape, BF16),
            jax.ShapeDtypeStruct(gate.shape, BF16),
            jax.ShapeDtypeStruct((weight.shape[0] // 2, channels * NY * NZ), BF16),
        ],
        scratch_shapes=[
            pltpu.SMEM(slots.shape, jnp.int32),
            pltpu.SemaphoreType.DMA((3,)),
            pltpu.SemaphoreType.DMA((BLOCKS,)),
        ],
        compiler_params=pltpu.CompilerParams(vmem_limit_bytes=8 << 20),
        name="fetch_weight",
    )(rate, residue, slots, query, gate, weight)


def mix_kernel(
    a0, a1, a3, a2, b0, b1, b3, b2, base_ref, bias_ref, pull_ref, rate_ref, query_ref, gate_ref, w0, w1,
    send_p, send_q, keep_p, keep_q, comb_scr,
):
    rows, channels = query_ref.shape
    modes = rate_ref.shape[0]
    heads = channels // HD
    first = (a0, a1, a3, a2)
    second = (b0, b1, b3, b2)
    rows_f = (lax.broadcasted_iota(jnp.int32, (8, HD), 0) + 1).astype(F32)
    scale = 1.0 / math.sqrt(HD)
    for h in range(heads):
        at = slice(h * HD, (h + 1) * HD)
        rate = rate_ref[:, at]
        pieces = [s[rows:, at].astype(F32) for pair in zip(first, second) for s in pair]
        entry = []
        for m in range(2):
            total = pull_ref[m, 0, :, at] * pieces[0]
            for i in range(1, 8):
                total = total + pull_ref[m, i, :, at] * pieces[i]
            entry.append(total)
        step8 = jnp.exp(-8.0 * rate)
        carry = [[jnp.zeros((8, HD), F32) for _ in range(8)] for _ in range(2)]
        for n in range(modes):
            term = jnp.exp(-rate[n : n + 1, :] * rows_f)
            factor = jnp.broadcast_to(step8[n : n + 1, :], (8, HD))
            wide = [jnp.broadcast_to(entry[m][n : n + 1, :], (8, HD)) for m in range(2)]
            for k in range(8):
                for m in range(2):
                    carry[m][k] = carry[m][k] + term * wide[m]
                if k < 7:
                    term = term * factor
        carried = jnp.concatenate([carry[m][k] for m in range(2) for k in range(8)], axis=0)
        hyena = gate_ref[:, at].astype(F32) * (base_ref[:, at] + carried)
        query = query_ref[:, at]
        scores = [
            lax.dot_general(query, k[:rows, at], (((1,), (1,)), ((), ())), preferred_element_type=F32) * scale
            + bias_ref[r]
            for r, k in enumerate(first)
        ]
        peak = jnp.maximum(jnp.maximum(scores[0], scores[1]), jnp.maximum(scores[2], scores[3]))
        peak = jnp.max(peak, axis=1, keepdims=True)
        probs = [jnp.exp(s - peak) for s in scores]
        total = jnp.sum((probs[0] + probs[1]) + (probs[2] + probs[3]), axis=1, keepdims=True)
        mixed = None
        for p, v in zip(probs, second):
            part = jnp.dot(p.astype(BF16), v[:rows, at], preferred_element_type=F32)
            mixed = part if mixed is None else mixed + part
        comb_scr[:, at] = (hyena + mixed / total).astype(BF16)
    comb = comb_scr[...]
    head = lax.axis_index("head")
    my_y, my_z = head // NZ, head % NZ
    for a, b in CHUNKS:
        chunk = (my_y ^ a) * NZ + (my_z ^ b)
        at = pl.ds(pl.multiple_of(chunk * channels, channels), channels)
        half = channels // 2
        part = jnp.dot(comb[:, :half], w0[:, at], preferred_element_type=F32)
        part = part + jnp.dot(comb[:, half:], w1[:, at], preferred_element_type=F32)
        for which, (send, keep) in enumerate(((send_p, keep_p), (send_q, keep_q))):
            orders = ORD_P if which == 0 else ORD_Q
            x = orders.index(a)
            y = orders.index(b)
            block = part[CH * which : CH * which + CH, :].astype(BF16)
            if x < 2:
                keep[x, y] = block
            else:
                send[x - 2, y] = block


def mix_stage(first, second, base, bias, pull, rate, query, gate, w0, w1):
    rows, channels = query.shape
    vmem = pl.BlockSpec(memory_space=pltpu.VMEM)
    return pl.pallas_call(
        mix_kernel,
        in_specs=[vmem] * 16,
        out_specs=[vmem] * 4,
        out_shape=[jax.ShapeDtypeStruct((2, 4, CH, channels), BF16)] * 4,
        scratch_shapes=[pltpu.VMEM((rows, channels), BF16)],
        compiler_params=pltpu.CompilerParams(vmem_limit_bytes=20 << 20),
        name="mix_project",
    )(*first, *second, base, bias, pull, rate, query, gate, w0, w1)


def swap(value, axis, mask):
    if axis == "ctx":
        pairs = [(i, i ^ mask) for i in range(4)]
        return lax.ppermute(value, "ctx", pairs)
    if axis == "y":
        pairs = [(y * NZ + z, (y ^ mask) * NZ + z) for y in range(NY) for z in range(NZ)]
    else:
        pairs = [(y * NZ + z, y * NZ + (z ^ mask)) for y in range(NY) for z in range(NZ)]
    return lax.ppermute(value, "head", pairs)


def body(
    stretch_slot, gate_in, conv_in, value_in, modal_rate, modal_residue, skip_gain, query_proj, key_proj, value_proj,
    out_weight,
):
    conv_in, value_in, key_proj, value_proj, query_proj, gate_in, out_weight, modal_rate, modal_residue = (
        pltpu.with_memory_space_constraint(x, pltpu.HBM)
        for x in (
            conv_in, value_in, key_proj, value_proj, query_proj, gate_in, out_weight, modal_rate, modal_residue
        )
    )
    slots = pltpu.with_memory_space_constraint(stretch_slot, pltpu.HBM)
    skip = pltpu.with_memory_space_constraint(skip_gain[None, :], pltpu.HBM)
    own_a, own_b, product, rate, residue, skip = pack_stage(
        conv_in, value_in, modal_rate, key_proj, value_proj, modal_residue, skip
    )

    def gather(value, mask):
        return swap(value, "ctx", mask)

    one_a = gather(own_a, 1)
    three_b = gather(own_b, 3)
    one_b = gather(own_b, 1)
    three_a = gather(own_a, 3)
    two_a = gather(one_a, 3)
    two_b = gather(three_b, 1)
    base, w0 = local_stage(product, rate, residue, skip, out_weight)
    bias, pull, query, gate, w1 = fetch_stage(rate, residue, slots, query_proj, gate_in, out_weight)
    send_p, send_q, keep_p, keep_q = mix_stage(
        (own_a, one_a, three_a, two_a), (own_b, one_b, three_b, two_b), base, bias, pull, rate, query, gate, w0, w1
    )

    def total(*terms):
        result = terms[0].astype(F32)
        for term in terms[1:]:
            result = result + term.astype(F32)
        return result.astype(BF16)

    keeps = (keep_p, keep_q)
    plans = ((("y", 1), ("y", 3), ("z", 1), ("z", 3)), (("y", 3), ("y", 1), ("z", 3), ("z", 1)))
    first = [swap(send, *plan[0]) for send, plan in zip((send_p, send_q), plans)]
    second = [swap(total(k[1], a[1]), *plan[1]) for k, a, plan in zip(keeps, first, plans)]
    third = [swap(total(k[0, 2:], a[0, 2:], b[2:]), *plan[2]) for k, a, b, plan in zip(keeps, first, second, plans)]
    fourth = [
        swap(total(k[0, 1], a[0, 1], b[1], c[1]), *plan[3])
        for k, a, b, c, plan in zip(keeps, first, second, third, plans)
    ]
    parts = [
        total(k[0, 0], a[0, 0], b[0], c[0], d) for k, a, b, c, d in zip(keeps, first, second, third, fourth)
    ]
    return jnp.concatenate(parts, axis=0)


def solution(mesh):
    return jax.shard_map(
        body,
        mesh=mesh,
        in_specs=(
            P("seq"),
            P(("seq", "ctx"), "head"),
            P(("seq", "ctx"), "head"),
            P(("seq", "ctx"), "head"),
            P("seq", "head"),
            P("seq", "head"),
            P(("seq", "head")),
            P(("seq", "ctx"), "head"),
            P(("seq", "ctx"), "head"),
            P(("seq", "ctx"), "head"),
            P(("seq", "head"), None),
        ),
        out_specs=P(("seq", "ctx"), "head"),
        check_vma=False,
    )
```

```python
import math

import jax
import jax.numpy as jnp
from jax import lax
from jax.experimental import pallas as pl
from jax.experimental.pallas import tpu as pltpu
from jax.sharding import PartitionSpec as P


HD = 128
CH = 64
NY = 4
NZ = 4
F32 = jnp.float32
BF16 = jnp.bfloat16
NEG = -1e30

STEPS = (4, 12, 1, 3)
CHAINS = ((48, (0, 1, 2, 3)), (48, (1, 0, 3, 2)), (16, (2, 3, 0, 1)), (16, (3, 2, 1, 0)))
CODES = [[(e >> (3 - r)) & 1 for r in range(4)] for e in range(15, -1, -1)]


def pack_kernel(
    conv_hbm, val_hbm, rate_hbm, key_hbm, value_hbm, res_hbm, skip_hbm,
    a_ref, b_ref, p_ref, rate_ref, res_ref, skip_ref, conv_scr, val_scr, sems,
):
    rows, channels = conv_scr.shape
    modes = rate_ref.shape[0]
    sources = (conv_hbm, val_hbm, rate_hbm, key_hbm, value_hbm, res_hbm, skip_hbm)
    targets = (
        conv_scr, val_scr, rate_ref, a_ref.at[pl.ds(0, rows), :], b_ref.at[pl.ds(0, rows), :], res_ref, skip_ref
    )
    copies = [pltpu.make_async_copy(s, t, sems.at[i]) for i, (s, t) in enumerate(zip(sources, targets))]
    for copy in copies:
        copy.start()
    for copy in copies[:3]:
        copy.wait()
    p_ref[...] = conv_scr[...].astype(F32) * val_scr[...].astype(F32)
    decay = jnp.exp(-rate_ref[...])
    states = [jnp.zeros((modes, channels), F32) for _ in range(2)]
    for j in range(CH):
        for m in range(2):
            states[m] = decay * states[m] + p_ref[m * CH + j : m * CH + j + 1, :]
    a_ref[rows:, :] = states[0].astype(BF16)
    b_ref[rows:, :] = states[1].astype(BF16)
    for copy in copies[3:]:
        copy.wait()


def pack_stage(conv_in, value_in, rate, keys, values, residue, skip):
    rows, channels = conv_in.shape
    modes = rate.shape[0]
    vmem = pl.BlockSpec(memory_space=pltpu.VMEM)
    hbm = pl.BlockSpec(memory_space=pltpu.HBM)
    return pl.pallas_call(
        pack_kernel,
        in_specs=[hbm] * 7,
        out_specs=[vmem] * 6,
        out_shape=[
            jax.ShapeDtypeStruct((rows + modes, channels), BF16),
            jax.ShapeDtypeStruct((rows + modes, channels), BF16),
            jax.ShapeDtypeStruct((rows, channels), F32),
            jax.ShapeDtypeStruct(rate.shape, F32),
            jax.ShapeDtypeStruct(residue.shape, F32),
            jax.ShapeDtypeStruct(skip.shape, F32),
        ],
        scratch_shapes=[
            pltpu.VMEM((rows, channels), BF16),
            pltpu.VMEM((rows, channels), BF16),
            pltpu.SemaphoreType.DMA((7,)),
        ],
        compiler_params=pltpu.CompilerParams(vmem_limit_bytes=4 << 20),
        name="pack_states",
    )(conv_in, value_in, rate, keys, values, residue, skip)


BLOCKS = 4


def weight_loads(weight_hbm, weight_ref, sems, start):
    block = weight_ref.shape[0] // BLOCKS
    loads = [
        pltpu.make_async_copy(
            weight_hbm.at[pl.ds(start + i * block, block), :], weight_ref.at[pl.ds(i * block, block), :], sems.at[i]
        )
        for i in range(BLOCKS)
    ]
    for load in loads:
        load.start()
    return loads


def local_kernel(p_ref, rate_ref, res_ref, skip_ref, weight_hbm, base_ref, weight_ref, h_scr, wsems):
    channels = p_ref.shape[1]
    modes = rate_ref.shape[0]
    heads = channels // HD
    loads = weight_loads(weight_hbm, weight_ref, wsems, 0)
    index = lax.broadcasted_iota(jnp.int32, (8, HD), 0)
    index_f = index.astype(F32)

    for h in range(heads):
        at = slice(h * HD, (h + 1) * HD)
        step8 = jnp.exp(-8.0 * rate_ref[:, at])
        taps = [jnp.zeros((8, HD), F32) for _ in range(8)]
        for n in range(modes):
            term = res_ref[n : n + 1, at] * jnp.exp(-rate_ref[n : n + 1, at] * index_f)
            factor = jnp.broadcast_to(step8[n : n + 1, :], (8, HD))
            for k in range(8):
                taps[k] = taps[k] + term
                if k < 7:
                    term = term * factor
        for s in range(8):
            previous = jnp.zeros((8, HD), F32)
            for k in range(8):
                if s == 0:
                    shifted = taps[k]
                else:
                    rolled = pltpu.roll(taps[k], s, 0)
                    shifted = jnp.where(index < s, previous, rolled)
                    previous = rolled
                h_scr[s * 64 + 8 * k : s * 64 + 8 * k + 8, :] = shifted
        skip = skip_ref[:, at]
        acc = [[jnp.zeros((8, HD), F32) for _ in range(8)] for _ in range(2)]
        for j in range(CH):
            jt, s = j // 8, j % 8
            wide = [jnp.broadcast_to(p_ref[m * CH + j : m * CH + j + 1, at], (8, HD)) for m in range(2)]
            for it in range(jt, 8):
                tap = h_scr[s * 64 + 8 * (it - jt) : s * 64 + 8 * (it - jt) + 8, :]
                for m in range(2):
                    acc[m][it] = acc[m][it] + tap * wide[m]
        for m in range(2):
            for it in range(8):
                row = m * CH + 8 * it
                base_ref[row : row + 8, at] = acc[m][it] + skip * p_ref[row : row + 8, at]
    for load in loads:
        load.wait()


def local_stage(product, rate, residue, skip, weight):
    vmem = pl.BlockSpec(memory_space=pltpu.VMEM)
    return pl.pallas_call(
        local_kernel,
        in_specs=[vmem] * 4 + [pl.BlockSpec(memory_space=pltpu.HBM)],
        out_specs=[vmem] * 2,
        out_shape=[
            jax.ShapeDtypeStruct(product.shape, F32),
            jax.ShapeDtypeStruct((weight.shape[0] // 2, weight.shape[1]), BF16),
        ],
        scratch_shapes=[pltpu.VMEM((512, HD), F32), pltpu.SemaphoreType.DMA((BLOCKS,))],
        compiler_params=pltpu.CompilerParams(vmem_limit_bytes=8 << 20),
        name="local_conv",
    )(product, rate, residue, skip, weight)


def fetch_kernel(
    rate_ref, res_ref, slot_hbm, query_hbm, gate_hbm, weight_hbm,
    bias_ref, pull_ref, query_ref, gate_ref, weight_ref, slot_ref, sems, wsems,
):
    rows = query_ref.shape[0]
    ctx = lax.axis_index("ctx")
    sources = (slot_hbm, query_hbm, gate_hbm)
    targets = (slot_ref, query_ref, gate_ref)
    copies = [pltpu.make_async_copy(s, t, sems.at[i]) for i, (s, t) in enumerate(zip(sources, targets))]
    for copy in copies:
        copy.start()
    loads = weight_loads(weight_hbm, weight_ref, wsems, weight_ref.shape[0])
    for copy in copies:
        copy.wait()
    key_st = [slot_ref[2 * (ctx ^ m) + s] for m in (0, 1, 3, 2) for s in range(2)]
    my_st = key_st[:2]
    col = lax.broadcasted_iota(jnp.int32, (rows, HD), 1)
    row = lax.broadcasted_iota(jnp.int32, (rows, HD), 0)
    q_pos = jnp.where(row < CH, my_st[0] * CH + row, my_st[1] * CH + row - CH)
    for r in range(4):
        k_pos = jnp.where(col < CH, key_st[2 * r] * CH + col, key_st[2 * r + 1] * CH + col - CH)
        bias_ref[r] = jnp.where(k_pos <= q_pos, 0.0, NEG)
    for m in range(2):
        for i, stretch in enumerate(key_st):
            gap = my_st[m] - 1 - stretch
            span = (CH * jnp.maximum(gap, 0)).astype(F32)
            pull_ref[m, i] = jnp.where(gap >= 0, 1.0, 0.0) * (res_ref[...] * jnp.exp(-rate_ref[...] * span))
    for load in loads:
        load.wait()


def fetch_stage(rate, residue, slots, query, gate, weight):
    rows, channels = query.shape
    vmem = pl.BlockSpec(memory_space=pltpu.VMEM)
    hbm = pl.BlockSpec(memory_space=pltpu.HBM)
    return pl.pallas_call(
        fetch_kernel,
        in_specs=[vmem] * 2 + [hbm] * 4,
        out_specs=[vmem] * 5,
        out_shape=[
            jax.ShapeDtypeStruct((4, rows, HD), F32),
            jax.ShapeDtypeStruct((2, 8) + rate.shape, F32),
            jax.ShapeDtypeStruct(query.shape, BF16),
            jax.ShapeDtypeStruct(gate.shape, BF16),
            jax.ShapeDtypeStruct((weight.shape[0] // 2, channels * NY * NZ), BF16),
        ],
        scratch_shapes=[
            pltpu.SMEM(slots.shape, jnp.int32),
            pltpu.SemaphoreType.DMA((3,)),
            pltpu.SemaphoreType.DMA((BLOCKS,)),
        ],
        compiler_params=pltpu.CompilerParams(vmem_limit_bytes=8 << 20),
        name="fetch_weight",
    )(rate, residue, slots, query, gate, weight)


def mix_kernel(
    a0, a1, a3, a2, b0, b1, b3, b2, base_ref, bias_ref, pull_ref, rate_ref, query_ref, gate_ref, w0, w1,
    *refs,
):
    sends, keeps, comb_scr = refs[: len(CHAINS)], refs[len(CHAINS) : 2 * len(CHAINS)], refs[-1]
    rows, channels = query_ref.shape
    modes = rate_ref.shape[0]
    heads = channels // HD
    first = (a0, a1, a3, a2)
    second = (b0, b1, b3, b2)
    rows_f = (lax.broadcasted_iota(jnp.int32, (8, HD), 0) + 1).astype(F32)
    scale = 1.0 / math.sqrt(HD)
    for h in range(heads):
        at = slice(h * HD, (h + 1) * HD)
        rate = rate_ref[:, at]
        pieces = [s[rows:, at].astype(F32) for pair in zip(first, second) for s in pair]
        entry = []
        for m in range(2):
            total = pull_ref[m, 0, :, at] * pieces[0]
            for i in range(1, 8):
                total = total + pull_ref[m, i, :, at] * pieces[i]
            entry.append(total)
        step8 = jnp.exp(-8.0 * rate)
        carry = [[jnp.zeros((8, HD), F32) for _ in range(8)] for _ in range(2)]
        for n in range(modes):
            term = jnp.exp(-rate[n : n + 1, :] * rows_f)
            factor = jnp.broadcast_to(step8[n : n + 1, :], (8, HD))
            wide = [jnp.broadcast_to(entry[m][n : n + 1, :], (8, HD)) for m in range(2)]
            for k in range(8):
                for m in range(2):
                    carry[m][k] = carry[m][k] + term * wide[m]
                if k < 7:
                    term = term * factor
        carried = jnp.concatenate([carry[m][k] for m in range(2) for k in range(8)], axis=0)
        hyena = gate_ref[:, at].astype(F32) * (base_ref[:, at] + carried)
        query = query_ref[:, at]
        scores = [
            lax.dot_general(query, k[:rows, at], (((1,), (1,)), ((), ())), preferred_element_type=F32) * scale
            + bias_ref[r]
            for r, k in enumerate(first)
        ]
        peak = jnp.maximum(jnp.maximum(scores[0], scores[1]), jnp.maximum(scores[2], scores[3]))
        peak = jnp.max(peak, axis=1, keepdims=True)
        probs = [jnp.exp(s - peak) for s in scores]
        total = jnp.sum((probs[0] + probs[1]) + (probs[2] + probs[3]), axis=1, keepdims=True)
        mixed = None
        for p, v in zip(probs, second):
            part = jnp.dot(p.astype(BF16), v[:rows, at], preferred_element_type=F32)
            mixed = part if mixed is None else mixed + part
        comb_scr[:, at] = (hyena + mixed / total).astype(BF16)
    comb = comb_scr[...]
    head = lax.axis_index("head")
    half = channels // 2
    for code in CODES:
        mask = 0
        for bit, step in zip(code, STEPS):
            mask ^= bit * step
        at = pl.ds(pl.multiple_of((head ^ mask) * channels, channels), channels)
        part = jnp.dot(comb[:, :half], w0[:, at], preferred_element_type=F32)
        part = part + jnp.dot(comb[:, half:], w1[:, at], preferred_element_type=F32)
        start = 0
        for (size, order), send, keep in zip(CHAINS, sends, keeps):
            bits = [code[r] for r in order]
            target = send if bits[0] else keep
            target[4 * bits[1] + 2 * bits[2] + bits[3]] = part[start : start + size, :].astype(BF16)
            start += size


def mix_stage(first, second, base, bias, pull, rate, query, gate, w0, w1):
    rows, channels = query.shape
    vmem = pl.BlockSpec(memory_space=pltpu.VMEM)
    return pl.pallas_call(
        mix_kernel,
        in_specs=[vmem] * 16,
        out_specs=[vmem] * (2 * len(CHAINS)),
        out_shape=[jax.ShapeDtypeStruct((8, size, channels), BF16) for size, _ in CHAINS] * 2,
        scratch_shapes=[pltpu.VMEM((rows, channels), BF16)],
        compiler_params=pltpu.CompilerParams(vmem_limit_bytes=20 << 20),
        name="mix_project",
    )(*first, *second, base, bias, pull, rate, query, gate, w0, w1)


def swap(value, mask):
    return lax.ppermute(value, "ctx", [(i, i ^ mask) for i in range(4)])


def halve(value, step):
    return lax.ppermute(value, "head", [(h, h ^ STEPS[step]) for h in range(NY * NZ)])


def body(
    stretch_slot, gate_in, conv_in, value_in, modal_rate, modal_residue, skip_gain, query_proj, key_proj, value_proj,
    out_weight,
):
    conv_in, value_in, key_proj, value_proj, query_proj, gate_in, out_weight, modal_rate, modal_residue = (
        pltpu.with_memory_space_constraint(x, pltpu.HBM)
        for x in (
            conv_in, value_in, key_proj, value_proj, query_proj, gate_in, out_weight, modal_rate, modal_residue
        )
    )
    slots = pltpu.with_memory_space_constraint(stretch_slot, pltpu.HBM)
    skip = pltpu.with_memory_space_constraint(skip_gain[None, :], pltpu.HBM)
    own_a, own_b, product, rate, residue, skip = pack_stage(
        conv_in, value_in, modal_rate, key_proj, value_proj, modal_residue, skip
    )

    one_a = swap(own_a, 1)
    three_b = swap(own_b, 3)
    one_b = swap(own_b, 1)
    three_a = swap(own_a, 3)
    two_a = swap(one_a, 3)
    two_b = swap(three_b, 1)
    base, w0 = local_stage(product, rate, residue, skip, out_weight)
    bias, pull, query, gate, w1 = fetch_stage(rate, residue, slots, query_proj, gate_in, out_weight)
    outs = mix_stage(
        (own_a, one_a, three_a, two_a), (own_b, one_b, three_b, two_b), base, bias, pull, rate, query, gate, w0, w1
    )

    def total(*terms):
        result = terms[0].astype(F32)
        for term in terms[1:]:
            result = result + term.astype(F32)
        return result.astype(BF16)

    count = len(CHAINS)
    sends, keeps, got = list(outs[:count]), outs[count:], [[] for _ in CHAINS]
    for r in range(4):
        for c in range(count):
            got[c].append(halve(sends[c], CHAINS[c][1][r]))
        size = 8 >> (r + 1)
        for c in range(count):
            terms = [keeps[c]] + got[c]
            sends[c] = total(*[t[size : 2 * size] if r < 3 else t[0] for t in terms])
    return jnp.concatenate(sends, axis=0)


def solution(mesh):
    return jax.shard_map(
        body,
        mesh=mesh,
        in_specs=(
            P("seq"),
            P(("seq", "ctx"), "head"),
            P(("seq", "ctx"), "head"),
            P(("seq", "ctx"), "head"),
            P("seq", "head"),
            P("seq", "head"),
            P(("seq", "head")),
            P(("seq", "ctx"), "head"),
            P(("seq", "ctx"), "head"),
            P(("seq", "ctx"), "head"),
            P(("seq", "head"), None),
        ),
        out_specs=P(("seq", "ctx"), "head"),
        check_vma=False,
    )
```

```python
import math

import jax
import jax.numpy as jnp
from jax import lax
from jax.experimental import pallas as pl
from jax.experimental.pallas import tpu as pltpu
from jax.sharding import PartitionSpec as P


HD = 128
CH = 64
NY = 4
NZ = 4
F32 = jnp.float32
BF16 = jnp.bfloat16
NEG = -1e30

STEPS = (4, 12, 1, 3)
CHAINS = ((48, (0, 1, 2, 3)), (48, (1, 0, 3, 2)), (16, (2, 3, 0, 1)), (16, (3, 2, 1, 0)))
CODES = [[(e >> (3 - r)) & 1 for r in range(4)] for e in range(15, -1, -1)]


def pack_kernel(
    conv_hbm, val_hbm, rate_hbm, key_hbm, value_hbm, res_hbm, skip_hbm,
    a_ref, b_ref, p_ref, rate_ref, res_ref, skip_ref, conv_scr, val_scr, sems,
):
    rows, channels = conv_scr.shape
    modes = rate_ref.shape[0]
    sources = (conv_hbm, val_hbm, rate_hbm, key_hbm, value_hbm, res_hbm, skip_hbm)
    targets = (
        conv_scr, val_scr, rate_ref, a_ref.at[pl.ds(0, rows), :], b_ref.at[pl.ds(0, rows), :], res_ref, skip_ref
    )
    copies = [pltpu.make_async_copy(s, t, sems.at[i]) for i, (s, t) in enumerate(zip(sources, targets))]
    for copy in copies:
        copy.start()
    for copy in copies[:3]:
        copy.wait()
    p_ref[...] = conv_scr[...].astype(F32) * val_scr[...].astype(F32)
    decay = jnp.exp(-rate_ref[...])
    states = [jnp.zeros((modes, channels), F32) for _ in range(2)]
    for j in range(CH):
        for m in range(2):
            states[m] = decay * states[m] + p_ref[m * CH + j : m * CH + j + 1, :]
    a_ref[rows:, :] = states[0].astype(BF16)
    b_ref[rows:, :] = states[1].astype(BF16)
    for copy in copies[3:]:
        copy.wait()


def pack_stage(conv_in, value_in, rate, keys, values, residue, skip):
    rows, channels = conv_in.shape
    modes = rate.shape[0]
    vmem = pl.BlockSpec(memory_space=pltpu.VMEM)
    hbm = pl.BlockSpec(memory_space=pltpu.HBM)
    return pl.pallas_call(
        pack_kernel,
        in_specs=[hbm] * 7,
        out_specs=[vmem] * 6,
        out_shape=[
            jax.ShapeDtypeStruct((rows + modes, channels), BF16),
            jax.ShapeDtypeStruct((rows + modes, channels), BF16),
            jax.ShapeDtypeStruct((rows, channels), F32),
            jax.ShapeDtypeStruct(rate.shape, F32),
            jax.ShapeDtypeStruct(residue.shape, F32),
            jax.ShapeDtypeStruct(skip.shape, F32),
        ],
        scratch_shapes=[
            pltpu.VMEM((rows, channels), BF16),
            pltpu.VMEM((rows, channels), BF16),
            pltpu.SemaphoreType.DMA((7,)),
        ],
        compiler_params=pltpu.CompilerParams(vmem_limit_bytes=4 << 20),
        name="pack_states",
    )(conv_in, value_in, rate, keys, values, residue, skip)


BLOCKS = 4


def weight_loads(weight_hbm, weight_ref, sems, start):
    block = weight_ref.shape[0] // BLOCKS
    loads = [
        pltpu.make_async_copy(
            weight_hbm.at[pl.ds(start + i * block, block), :], weight_ref.at[pl.ds(i * block, block), :], sems.at[i]
        )
        for i in range(BLOCKS)
    ]
    for load in loads:
        load.start()
    return loads


def local_kernel(p_ref, rate_ref, res_ref, skip_ref, weight_hbm, base_ref, weight_ref, h_scr, wsems):
    channels = p_ref.shape[1]
    modes = rate_ref.shape[0]
    heads = channels // HD
    loads = weight_loads(weight_hbm, weight_ref, wsems, 0)
    index = lax.broadcasted_iota(jnp.int32, (8, HD), 0)
    index_f = index.astype(F32)

    for h in range(heads):
        at = slice(h * HD, (h + 1) * HD)
        step8 = jnp.exp(-8.0 * rate_ref[:, at])
        taps = [jnp.zeros((8, HD), F32) for _ in range(8)]
        for n in range(modes):
            term = res_ref[n : n + 1, at] * jnp.exp(-rate_ref[n : n + 1, at] * index_f)
            factor = jnp.broadcast_to(step8[n : n + 1, :], (8, HD))
            for k in range(8):
                taps[k] = taps[k] + term
                if k < 7:
                    term = term * factor
        for s in range(8):
            previous = jnp.zeros((8, HD), F32)
            for k in range(8):
                if s == 0:
                    shifted = taps[k]
                else:
                    rolled = pltpu.roll(taps[k], s, 0)
                    shifted = jnp.where(index < s, previous, rolled)
                    previous = rolled
                h_scr[s * 64 + 8 * k : s * 64 + 8 * k + 8, :] = shifted
        skip = skip_ref[:, at]
        acc = [[jnp.zeros((8, HD), F32) for _ in range(8)] for _ in range(2)]
        for j in range(CH):
            jt, s = j // 8, j % 8
            wide = [jnp.broadcast_to(p_ref[m * CH + j : m * CH + j + 1, at], (8, HD)) for m in range(2)]
            for it in range(jt, 8):
                tap = h_scr[s * 64 + 8 * (it - jt) : s * 64 + 8 * (it - jt) + 8, :]
                for m in range(2):
                    acc[m][it] = acc[m][it] + tap * wide[m]
        for m in range(2):
            for it in range(8):
                row = m * CH + 8 * it
                base_ref[row : row + 8, at] = acc[m][it] + skip * p_ref[row : row + 8, at]
    for load in loads:
        load.wait()


def local_stage(product, rate, residue, skip, weight):
    vmem = pl.BlockSpec(memory_space=pltpu.VMEM)
    return pl.pallas_call(
        local_kernel,
        in_specs=[vmem] * 4 + [pl.BlockSpec(memory_space=pltpu.HBM)],
        out_specs=[vmem] * 2,
        out_shape=[
            jax.ShapeDtypeStruct(product.shape, F32),
            jax.ShapeDtypeStruct((weight.shape[0] // 2, weight.shape[1]), BF16),
        ],
        scratch_shapes=[pltpu.VMEM((512, HD), F32), pltpu.SemaphoreType.DMA((BLOCKS,))],
        compiler_params=pltpu.CompilerParams(vmem_limit_bytes=8 << 20),
        name="local_conv",
    )(product, rate, residue, skip, weight)


def fetch_kernel(
    rate_ref, res_ref, slot_hbm, query_hbm, gate_hbm, weight_hbm,
    bias_ref, pull_ref, query_ref, gate_ref, weight_ref, slot_ref, sems, wsems,
):
    rows = query_ref.shape[0]
    ctx = lax.axis_index("ctx")
    sources = (slot_hbm, query_hbm, gate_hbm)
    targets = (slot_ref, query_ref, gate_ref)
    copies = [pltpu.make_async_copy(s, t, sems.at[i]) for i, (s, t) in enumerate(zip(sources, targets))]
    for copy in copies:
        copy.start()
    loads = weight_loads(weight_hbm, weight_ref, wsems, weight_ref.shape[0])
    for copy in copies:
        copy.wait()
    key_st = [slot_ref[2 * (ctx ^ m) + s] for m in (0, 1, 3, 2) for s in range(2)]
    my_st = key_st[:2]
    col = lax.broadcasted_iota(jnp.int32, (rows, HD), 1)
    row = lax.broadcasted_iota(jnp.int32, (rows, HD), 0)
    q_pos = jnp.where(row < CH, my_st[0] * CH + row, my_st[1] * CH + row - CH)
    for r in range(4):
        k_pos = jnp.where(col < CH, key_st[2 * r] * CH + col, key_st[2 * r + 1] * CH + col - CH)
        bias_ref[r] = jnp.where(k_pos <= q_pos, 0.0, NEG)
    for m in range(2):
        for i, stretch in enumerate(key_st):
            gap = my_st[m] - 1 - stretch
            span = (CH * jnp.maximum(gap, 0)).astype(F32)
            pull_ref[m, i] = jnp.where(gap >= 0, 1.0, 0.0) * (res_ref[...] * jnp.exp(-rate_ref[...] * span))
    for load in loads:
        load.wait()


def fetch_stage(rate, residue, slots, query, gate, weight):
    rows, channels = query.shape
    vmem = pl.BlockSpec(memory_space=pltpu.VMEM)
    hbm = pl.BlockSpec(memory_space=pltpu.HBM)
    return pl.pallas_call(
        fetch_kernel,
        in_specs=[vmem] * 2 + [hbm] * 4,
        out_specs=[vmem] * 5,
        out_shape=[
            jax.ShapeDtypeStruct((4, rows, HD), F32),
            jax.ShapeDtypeStruct((2, 8) + rate.shape, F32),
            jax.ShapeDtypeStruct(query.shape, BF16),
            jax.ShapeDtypeStruct(gate.shape, BF16),
            jax.ShapeDtypeStruct((weight.shape[0] // 2, channels * NY * NZ), BF16),
        ],
        scratch_shapes=[
            pltpu.SMEM(slots.shape, jnp.int32),
            pltpu.SemaphoreType.DMA((3,)),
            pltpu.SemaphoreType.DMA((BLOCKS,)),
        ],
        compiler_params=pltpu.CompilerParams(vmem_limit_bytes=8 << 20),
        name="fetch_weight",
    )(rate, residue, slots, query, gate, weight)


def mix_kernel(
    a0, a1, a3, a2, b0, b1, b3, b2, base_ref, bias_ref, pull_ref, rate_ref, query_ref, gate_ref, w0, w1,
    *refs,
):
    sends, keeps, comb_scr = refs[: len(CHAINS)], refs[len(CHAINS) : 2 * len(CHAINS)], refs[-1]
    rows, channels = query_ref.shape
    modes = rate_ref.shape[0]
    heads = channels // HD
    first = (a0, a1, a3, a2)
    second = (b0, b1, b3, b2)
    rows_f = (lax.broadcasted_iota(jnp.int32, (8, HD), 0) + 1).astype(F32)
    scale = 1.0 / math.sqrt(HD)
    for h in range(heads):
        at = slice(h * HD, (h + 1) * HD)
        rate = rate_ref[:, at]
        pieces = [s[rows:, at].astype(F32) for pair in zip(first, second) for s in pair]
        entry = []
        for m in range(2):
            total = pull_ref[m, 0, :, at] * pieces[0]
            for i in range(1, 8):
                total = total + pull_ref[m, i, :, at] * pieces[i]
            entry.append(total)
        step8 = jnp.exp(-8.0 * rate)
        carry = [[jnp.zeros((8, HD), F32) for _ in range(8)] for _ in range(2)]
        for n in range(modes):
            term = jnp.exp(-rate[n : n + 1, :] * rows_f)
            factor = jnp.broadcast_to(step8[n : n + 1, :], (8, HD))
            wide = [jnp.broadcast_to(entry[m][n : n + 1, :], (8, HD)) for m in range(2)]
            for k in range(8):
                for m in range(2):
                    carry[m][k] = carry[m][k] + term * wide[m]
                if k < 7:
                    term = term * factor
        carried = jnp.concatenate([carry[m][k] for m in range(2) for k in range(8)], axis=0)
        hyena = gate_ref[:, at].astype(F32) * (base_ref[:, at] + carried)
        query = query_ref[:, at]
        scores = [
            lax.dot_general(query, k[:rows, at], (((1,), (1,)), ((), ())), preferred_element_type=F32) * scale
            + bias_ref[r]
            for r, k in enumerate(first)
        ]
        peak = jnp.maximum(jnp.maximum(scores[0], scores[1]), jnp.maximum(scores[2], scores[3]))
        peak = jnp.max(peak, axis=1, keepdims=True)
        probs = [jnp.exp(s - peak) for s in scores]
        total = jnp.sum((probs[0] + probs[1]) + (probs[2] + probs[3]), axis=1, keepdims=True)
        mixed = None
        for p, v in zip(probs, second):
            part = jnp.dot(p.astype(BF16), v[:rows, at], preferred_element_type=F32)
            mixed = part if mixed is None else mixed + part
        comb_scr[:, at] = (hyena + mixed / total).astype(BF16)
    comb = comb_scr[...]
    head = lax.axis_index("head")
    half = channels // 2
    for code in CODES:
        mask = 0
        for bit, step in zip(code, STEPS):
            mask ^= bit * step
        at = pl.ds(pl.multiple_of((head ^ mask) * channels, channels), channels)
        part = jnp.dot(comb[:, :half], w0[:, at], preferred_element_type=F32)
        part = part + jnp.dot(comb[:, half:], w1[:, at], preferred_element_type=F32)
        start = 0
        for (size, order), send, keep in zip(CHAINS, sends, keeps):
            bits = [code[r] for r in order]
            target = send if bits[0] else keep
            target[4 * bits[1] + 2 * bits[2] + bits[3]] = part[start : start + size, :].astype(BF16)
            start += size


def mix_stage(first, second, base, bias, pull, rate, query, gate, w0, w1):
    rows, channels = query.shape
    vmem = pl.BlockSpec(memory_space=pltpu.VMEM)
    return pl.pallas_call(
        mix_kernel,
        in_specs=[vmem] * 16,
        out_specs=[vmem] * (2 * len(CHAINS)),
        out_shape=[jax.ShapeDtypeStruct((8, size, channels), BF16) for size, _ in CHAINS] * 2,
        scratch_shapes=[pltpu.VMEM((rows, channels), BF16)],
        compiler_params=pltpu.CompilerParams(vmem_limit_bytes=20 << 20),
        name="mix_project",
    )(*first, *second, base, bias, pull, rate, query, gate, w0, w1)


def last_kernel(*refs):
    start = 0
    for c, (size, _) in enumerate(CHAINS):
        result = refs[5 * c][0].astype(F32)
        for ref in refs[5 * c + 1 : 5 * c + 5]:
            result = result + ref[0].astype(F32)
        refs[-1][start : start + size, :] = result.astype(BF16)
        start += size


def last_stage(terms, rows, channels):
    vmem = pl.BlockSpec(memory_space=pltpu.VMEM)
    return pl.pallas_call(
        last_kernel,
        in_specs=[vmem] * len(terms),
        out_specs=vmem,
        out_shape=jax.ShapeDtypeStruct((rows, channels), BF16),
        compiler_params=pltpu.CompilerParams(vmem_limit_bytes=4 << 20),
        name="last_sum",
    )(*terms)


def swap(value, mask):
    return lax.ppermute(value, "ctx", [(i, i ^ mask) for i in range(4)])


def halve(value, step):
    return lax.ppermute(value, "head", [(h, h ^ STEPS[step]) for h in range(NY * NZ)])


def body(
    stretch_slot, gate_in, conv_in, value_in, modal_rate, modal_residue, skip_gain, query_proj, key_proj, value_proj,
    out_weight,
):
    conv_in, value_in, key_proj, value_proj, query_proj, gate_in, out_weight, modal_rate, modal_residue = (
        pltpu.with_memory_space_constraint(x, pltpu.HBM)
        for x in (
            conv_in, value_in, key_proj, value_proj, query_proj, gate_in, out_weight, modal_rate, modal_residue
        )
    )
    slots = pltpu.with_memory_space_constraint(stretch_slot, pltpu.HBM)
    skip = pltpu.with_memory_space_constraint(skip_gain[None, :], pltpu.HBM)
    own_a, own_b, product, rate, residue, skip = pack_stage(
        conv_in, value_in, modal_rate, key_proj, value_proj, modal_residue, skip
    )

    one_a = swap(own_a, 1)
    three_b = swap(own_b, 3)
    one_b = swap(own_b, 1)
    three_a = swap(own_a, 3)
    two_a = swap(one_a, 3)
    two_b = swap(three_b, 1)
    base, w0 = local_stage(product, rate, residue, skip, out_weight)
    bias, pull, query, gate, w1 = fetch_stage(rate, residue, slots, query_proj, gate_in, out_weight)
    outs = mix_stage(
        (own_a, one_a, three_a, two_a), (own_b, one_b, three_b, two_b), base, bias, pull, rate, query, gate, w0, w1
    )

    def total(*terms):
        result = terms[0].astype(F32)
        for term in terms[1:]:
            result = result + term.astype(F32)
        return result.astype(BF16)

    count = len(CHAINS)
    sends, keeps, got = list(outs[:count]), outs[count:], [[] for _ in CHAINS]
    for r in range(4):
        for c in range(count):
            got[c].append(halve(sends[c], CHAINS[c][1][r]))
        size = 8 >> (r + 1)
        if r == 3:
            break
        for c in range(count):
            terms = [keeps[c]] + got[c]
            sends[c] = total(*[t[size : 2 * size] for t in terms])
    terms = [term for c in range(count) for term in [keeps[c]] + got[c]]
    return last_stage(terms, *query_proj.shape)


def solution(mesh):
    return jax.shard_map(
        body,
        mesh=mesh,
        in_specs=(
            P("seq"),
            P(("seq", "ctx"), "head"),
            P(("seq", "ctx"), "head"),
            P(("seq", "ctx"), "head"),
            P("seq", "head"),
            P("seq", "head"),
            P(("seq", "head")),
            P(("seq", "ctx"), "head"),
            P(("seq", "ctx"), "head"),
            P(("seq", "ctx"), "head"),
            P(("seq", "head"), None),
        ),
        out_specs=P(("seq", "ctx"), "head"),
        check_vma=False,
    )
```
